1024 devices in a mesh: energy: 64 (over z_hi, y, core), mom: 16 (over z_lo, x).
Axes of the slice: x: 8, y: 8, z: 8 (z_hi: 4, z_lo: 2; z = z_hi * 2 + z_lo), core: 2. Of those that a mesh axis runs over, the one named last changes fastest.
Arguments:
- green: bfloat16 [16, 64, 4, 2, 256, 256], P('mom', 'energy'), may hold values from -6 to 6
- coupling: bfloat16 [2, 256, 256], replicated, may hold values from -0.375 to 0.375
- phonon: bfloat16 [3, 1024, 256], replicated, may hold values from -4 to 4
- shift: int32 [3, 2], replicated, may hold values from 0 to 1
Outputs:
- sigma: bfloat16 [16, 64, 4, 2, 256, 256], P('mom', 'energy')
The draws below stay inside these ranges and needn't reach their ends.
All inputs are finite; a program needn't handle non-finite values.
Results may differ from the reference program's by a relative error of at most 0.0049.
Values may be sent and summed in bfloat16 or wider, within the bound.
A program may use at most 64 MiB of HBM per device.

```python
import jax
import jax.numpy as jnp
from jax import lax

NO = 256
MODES = 2
QR = 1
SMAX = 1
E_OUT = 4
NOFF = 3
NK = 16
NG = 64


def draw_shift(key, part):
    first_key, second_key = jax.random.split(jax.random.fold_in(key, 11))
    values_flat = jax.random.randint(first_key, (NOFF * MODES,), 0, SMAX + 1, dtype=jnp.int32)
    placing = jax.random.permutation(second_key, NOFF * MODES)
    values_flat = values_flat.at[placing[0]].set(SMAX).at[placing[1]].set(0)
    return values_flat.reshape(NOFF, MODES)


def steps_of(own_key, shape, shards, low, high):
    level, own = 1.0, jax.random.fold_in(own_key, 6)
    for dim, blocks in shards:
        steps = jnp.exp(jax.random.uniform(jax.random.fold_in(own, dim), (blocks,), jnp.float32, low / len(shards), high / len(shards)))
        level = level * jnp.repeat(steps, shape[dim] // blocks).reshape([-1 if axis == dim else 1 for axis in range(len(shape))])
    return level


def normal_values(rng, shape, deviation, limit, shards=(), kind=jnp.bfloat16):
    drawn = jax.random.normal(rng, shape, jnp.float32) * deviation
    if len(shards) > 0:
        drawn = steps_of(rng, shape, shards, -0.22, 0.18) * drawn
    return jnp.clip(drawn, min=-limit, max=limit).astype(kind)


def setup_inputs(seed: int = 0) -> dict:
    streams_of = jax.random.split(jax.random.key(seed), 5)
    green = normal_values(streams_of[0], (NK, NG, E_OUT, 2, NO, NO), 1.0, 6.0, ((0, 16), (1, 64)))
    coupling = normal_values(streams_of[1], (MODES, NO, NO), NO ** -0.5, 0.375)
    phonon = normal_values(streams_of[2], (NOFF, MODES * 2 * NO, NO), 0.5, 4.0)
    shift = draw_shift(jax.random.fold_in(streams_of[4], 71), 0)
    return dict(green=green, coupling=coupling, phonon=phonon, shift=shift)


def reference(green, coupling, phonon, shift):
    points = green.shape[0]
    groups = green.shape[1]
    couple = coupling.astype(jnp.float32)

    def one_point(momentum):
        accumulated = jnp.zeros((groups, E_OUT, 2, NO, NO), jnp.float32)
        for offset in range(2 * QR + 1):
            source = ((momentum - (offset - QR)) % points).astype(jnp.int32)
            blocks = lax.dynamic_index_in_dim(green, source, 0, keepdims=False)
            flat = blocks.reshape(groups * E_OUT, 2, NO, NO)
            padded = jnp.concatenate([jnp.zeros((SMAX, 2, NO, NO), flat.dtype), flat], axis=0)
            weights = phonon[offset].astype(jnp.float32).reshape(MODES, 2, NO, NO)
            for mode_index in range(MODES):
                first_slot = (SMAX - shift[offset, mode_index]).astype(jnp.int32)
                window = lax.dynamic_slice_in_dim(padded, first_slot, groups * E_OUT, 0)
                window = window.reshape(groups, E_OUT, 2, NO, NO).astype(jnp.float32)
                left_product = jnp.einsum('xy,gecyz->gecxz', couple[mode_index], window).astype(jnp.bfloat16)
                left_product = lax.optimization_barrier(left_product).astype(jnp.float32)
                product = jnp.einsum('gecxy,yz->gecxz', left_product, couple[mode_index])
                real_part = product[:, :, 0] * weights[mode_index, 0] - product[:, :, 1] * weights[mode_index, 1]
                imag_part = product[:, :, 0] * weights[mode_index, 1] + product[:, :, 1] * weights[mode_index, 0]
                accumulated = accumulated + jnp.stack([real_part, imag_part], axis=2)
        return accumulated.astype(jnp.bfloat16)

    return lax.map(one_point, jnp.arange(points, dtype=jnp.int32))
```

```python
import jax
import jax.numpy as jnp
from jax import lax
from jax.experimental import pallas as pl
from jax.experimental.pallas import tpu as pltpu
from jax.sharding import PartitionSpec as P

NO = 256
MODES = 2
E_OUT = 4
NOFF = 3
HALF = 128
STEP = 16
VMEM_LIMIT = 24 * 1024 * 1024
MESH = pl.DeviceIdType.MESH

CHUNKS = [(1, 0), (1, 1), (2, 0), (2, 1), (3, 0), (3, 1), (0, 0), (0, 1)]


def kernel(
    green, coupling, phonon, shift_in, out,
    shift, slots, couple, weights, prod, to_left, to_right, from_right, from_left, own,
    in_sem, below_sem, left_send, left_recv, right_send, right_recv,
):
    me = lax.axis_index("mom")
    points = lax.axis_size("mom")
    group = lax.axis_index("energy")
    groups = lax.axis_size("energy")
    left = lax.rem(me + points - 1, points)
    right = lax.rem(me + 1, points)
    has_below = group > 0
    has_above = group < groups - 1

    barrier = pltpu.get_barrier_semaphore()
    pl.semaphore_signal(barrier, inc=1, device_id={"mom": left}, device_id_type=MESH)
    pl.semaphore_signal(barrier, inc=1, device_id={"mom": right}, device_id_type=MESH)

    @pl.when(has_above)
    def _():
        pl.semaphore_signal(barrier, inc=1, device_id={"energy": group + 1}, device_id_type=MESH)

    @pl.when(has_below)
    def _():
        pl.semaphore_signal(barrier, inc=1, device_id={"energy": group - 1}, device_id_type=MESH)

    loads = {"shift": pltpu.make_async_copy(shift_in, shift, in_sem.at[E_OUT + 1 + NOFF])}
    loads["couple"] = pltpu.make_async_copy(coupling, couple, in_sem.at[0])
    for s in range(E_OUT):
        loads[s + 1] = pltpu.make_async_copy(green.at[s], slots.at[s + 1], in_sem.at[s + 1])
    for j in range(NOFF):
        loads["w", j] = pltpu.make_async_copy(phonon.at[j], weights.at[j], in_sem.at[E_OUT + 1 + j])
    order = ["shift", "couple", 1, 2, ("w", 0), ("w", 2), ("w", 1), 3, 4]
    for name in order:
        loads[name].start()
    waited = set()

    def need(name):
        if name not in waited:
            waited.add(name)
            loads[name].wait()

    below = pltpu.make_async_remote_copy(
        src_ref=green.at[E_OUT - 1],
        dst_ref=slots.at[0],
        send_sem=below_sem.at[0],
        recv_sem=below_sem.at[1],
        device_id={"energy": lax.rem(group + 1, groups)},
        device_id_type=MESH,
    )

    def products(s, half):
        rows = pl.ds(half * HALF, HALF)
        stacked = couple[:, rows, :].reshape(MODES * HALF, NO)
        for c in range(2):
            lefts = jnp.dot(stacked, slots[s, c], preferred_element_type=jnp.float32)
            lefts = lefts.astype(jnp.bfloat16)
            for a in range(MODES):
                prod[s, a, c, rows, :] = jnp.dot(
                    lefts[a * HALF:(a + 1) * HALF], couple[a], preferred_element_type=jnp.float32
                )

    def term(j, i, r):
        re = im = None
        for a in range(MODES):
            s = i + 1 - shift[a, j]
            p0 = prod[s, a, 0, pl.ds(r, STEP), :]
            p1 = prod[s, a, 1, pl.ds(r, STEP), :]
            d0 = weights[j, pl.ds(2 * a * NO + r, STEP), :].astype(jnp.float32)
            d1 = weights[j, pl.ds((2 * a + 1) * NO + r, STEP), :].astype(jnp.float32)
            one, two = p0 * d0 - p1 * d1, p0 * d1 + p1 * d0
            re = one if re is None else re + one
            im = two if im is None else im + two
        return re, im

    def over_rows(half, fn):
        def step(n, carry):
            fn(pl.multiple_of(half * HALF + n * STEP, STEP))
            return carry
        lax.fori_loop(0, HALF // STEP, step, 0)

    def sends(n, i, half):
        rows = pl.ds(half * HALF, HALF)
        a = pltpu.make_async_remote_copy(
            src_ref=to_left.at[i, :, rows, :], dst_ref=from_right.at[i, :, rows, :],
            send_sem=left_send.at[n], recv_sem=left_recv.at[n],
            device_id={"mom": left}, device_id_type=MESH)
        b = pltpu.make_async_remote_copy(
            src_ref=to_right.at[i, :, rows, :], dst_ref=from_left.at[i, :, rows, :],
            send_sem=right_send.at[n], recv_sem=right_recv.at[n],
            device_id={"mom": right}, device_id_type=MESH)
        return a, b

    have = set()
    copies = []
    for n, (i, half) in enumerate(CHUNKS):
        for s in (i + 1, i):
            if (s, half) in have:
                continue
            have.add((s, half))
            need("couple")
            if s > 0:
                need(s)
            elif half == 0:
                @pl.when(has_below)
                def _():
                    below.wait_recv()
            products(s, half)

        need("shift")
        need(("w", 0))
        need(("w", 2))

        def outer(r, i=i):
            re, im = term(0, i, r)
            to_left[i, 0, pl.ds(r, STEP), :] = re.astype(jnp.bfloat16)
            to_left[i, 1, pl.ds(r, STEP), :] = im.astype(jnp.bfloat16)
            re, im = term(2, i, r)
            to_right[i, 0, pl.ds(r, STEP), :] = re.astype(jnp.bfloat16)
            to_right[i, 1, pl.ds(r, STEP), :] = im.astype(jnp.bfloat16)

        over_rows(half, outer)

        need(("w", 1))

        def inner(r, i=i):
            re, im = term(1, i, r)
            own[i, 0, pl.ds(r, STEP), :] = re
            own[i, 1, pl.ds(r, STEP), :] = im

        if n > 0:
            over_rows(half, inner)
        else:
            pl.semaphore_wait(barrier, 2 + has_below.astype(jnp.int32) + has_above.astype(jnp.int32))

            @pl.when(has_above)
            def _():
                below.start()

            @pl.when(jnp.logical_not(has_below))
            def _():
                slots[0] = jnp.zeros((2, NO, NO), jnp.bfloat16)

        pair = sends(n, i, half)
        for copy in pair:
            copy.start()
        copies.append(pair)
        if n == 0:
            over_rows(half, inner)

    for n, (i, half) in enumerate(CHUNKS):
        for copy in copies[n]:
            copy.wait_recv()

        def final(r, i=i):
            for c in range(2):
                rows = pl.ds(r, STEP)
                total = own[i, c, rows, :] + from_right[i, c, rows, :].astype(jnp.float32)
                total = total + from_left[i, c, rows, :].astype(jnp.float32)
                out[i, c, rows, :] = total.astype(jnp.bfloat16)

        over_rows(half, final)

    for pair in copies:
        for copy in pair:
            copy.wait_send()

    @pl.when(has_above)
    def _():
        below.wait_send()


def body(green, coupling, phonon, shift):
    block = (E_OUT, 2, NO, NO)
    n = len(CHUNKS)
    result = pl.pallas_call(
        kernel,
        out_shape=jax.ShapeDtypeStruct(block, jnp.bfloat16),
        in_specs=[pl.BlockSpec(memory_space=pltpu.HBM)] * 4,
        out_specs=pl.BlockSpec(memory_space=pltpu.VMEM),
        scratch_shapes=[
            pltpu.SMEM((MODES, NOFF), jnp.int32),
            pltpu.VMEM((E_OUT + 1, 2, NO, NO), jnp.bfloat16),
            pltpu.VMEM((MODES, NO, NO), jnp.bfloat16),
            pltpu.VMEM((NOFF, MODES * 2 * NO, NO), jnp.bfloat16),
            pltpu.VMEM((E_OUT + 1, MODES, 2, NO, NO), jnp.float32),
            pltpu.VMEM(block, jnp.bfloat16),
            pltpu.VMEM(block, jnp.bfloat16),
            pltpu.VMEM(block, jnp.bfloat16),
            pltpu.VMEM(block, jnp.bfloat16),
            pltpu.VMEM(block, jnp.float32),
            pltpu.SemaphoreType.DMA((E_OUT + 2 + NOFF,)),
            pltpu.SemaphoreType.DMA((2,)),
            pltpu.SemaphoreType.DMA((n,)),
            pltpu.SemaphoreType.DMA((n,)),
            pltpu.SemaphoreType.DMA((n,)),
            pltpu.SemaphoreType.DMA((n,)),
        ],
        compiler_params=pltpu.CompilerParams(
            collective_id=0, has_side_effects=True, vmem_limit_bytes=VMEM_LIMIT
        ),
    )(
        pltpu.with_memory_space_constraint(green.reshape(block), pltpu.HBM),
        pltpu.with_memory_space_constraint(coupling, pltpu.HBM),
        pltpu.with_memory_space_constraint(phonon, pltpu.HBM),
        pltpu.with_memory_space_constraint(shift.T, pltpu.HBM),
    )
    return result.reshape((1, 1) + block)


def solution(mesh):
    placed = (P("mom", "energy", None, None, None, None), P(), P(), P())
    return jax.shard_map(
        body,
        mesh=mesh,
        in_specs=placed,
        out_specs=P("mom", "energy", None, None, None, None),
        check_vma=False,
    )
```

```python
import jax
import jax.numpy as jnp
from jax import lax
from jax.experimental import pallas as pl
from jax.experimental.pallas import tpu as pltpu
from jax.sharding import PartitionSpec as P

NO = 256
MODES = 2
E_OUT = 4
NOFF = 3
HALF = 128
STEP = 16
EDGE = 16
DETOUR = 3
VMEM_LIMIT = 24 * 1024 * 1024
MESH = pl.DeviceIdType.MESH

CHUNKS = [(1, 0), (1, 1), (2, 0), (2, 1), (3, 0), (3, 1), (0, 0), (0, 1)]


def kernel(
    green, coupling, phonon, shift_in, out,
    shift, slots, couple, weights, prod, to_left, to_right, from_right, from_left, own,
    relay, in_sem, below_sem, relay_sem, left_send, left_recv, right_send, right_recv,
):
    me = lax.axis_index("mom")
    points = lax.axis_size("mom")
    group = lax.axis_index("energy")
    groups = lax.axis_size("energy")
    left = lax.rem(me + points - 1, points)
    right = lax.rem(me + 1, points)
    has_below = group > 0
    has_above = group < groups - 1

    detoured = (me == points // 2 - 1) | (me == points // 2)
    place = lax.rem(group, EDGE)
    detour_up = detoured & has_above & (place == EDGE - 1)
    detour_over = detoured & (group >= EDGE) & (place == DETOUR - 1)
    detour_down = detoured & has_below & (place == 0)
    direct_up = has_above & jnp.logical_not(detour_up)
    direct_down = has_below & jnp.logical_not(detour_down)
    over = lax.rem(group + DETOUR, groups)

    barrier = pltpu.get_barrier_semaphore()
    pl.semaphore_signal(barrier, inc=1, device_id={"mom": left}, device_id_type=MESH)
    pl.semaphore_signal(barrier, inc=1, device_id={"mom": right}, device_id_type=MESH)

    @pl.when(direct_down)
    def _():
        pl.semaphore_signal(barrier, inc=1, device_id={"energy": group - 1}, device_id_type=MESH)

    @pl.when(detour_over)
    def _():
        pl.semaphore_signal(barrier, inc=1, device_id={"energy": group - DETOUR}, device_id_type=MESH)

    @pl.when(detour_down)
    def _():
        pl.semaphore_signal(barrier, inc=1, device_id={"energy": group + DETOUR - 1}, device_id_type=MESH)

    loads = {"shift": pltpu.make_async_copy(shift_in, shift, in_sem.at[E_OUT + 1 + NOFF])}
    loads["couple"] = pltpu.make_async_copy(coupling, couple, in_sem.at[0])
    for s in range(E_OUT):
        loads[s + 1] = pltpu.make_async_copy(green.at[s], slots.at[s + 1], in_sem.at[s + 1])
    for j in range(NOFF):
        loads["w", j] = pltpu.make_async_copy(phonon.at[j], weights.at[j], in_sem.at[E_OUT + 1 + j])
    order = ["shift", "couple", 1, 2, ("w", 0), ("w", 2), ("w", 1), 3, 4]
    for name in order:
        loads[name].start()
    waited = set()

    def need(name):
        if name not in waited:
            waited.add(name)
            loads[name].wait()

    below = pltpu.make_async_remote_copy(
        src_ref=green.at[E_OUT - 1],
        dst_ref=slots.at[0],
        send_sem=below_sem.at[0],
        recv_sem=below_sem.at[1],
        device_id={"energy": lax.rem(group + 1, groups)},
        device_id_type=MESH,
    )

    out_of_way = pltpu.make_async_remote_copy(
        src_ref=green.at[E_OUT - 1],
        dst_ref=relay,
        send_sem=relay_sem.at[0],
        recv_sem=relay_sem.at[1],
        device_id={"energy": over},
        device_id_type=MESH,
    )
    back = pltpu.make_async_remote_copy(
        src_ref=relay,
        dst_ref=slots.at[0],
        send_sem=relay_sem.at[2],
        recv_sem=below_sem.at[1],
        device_id={"energy": lax.rem(group + groups - DETOUR + 1, groups)},
        device_id_type=MESH,
    )

    def products(s, half):
        rows = pl.ds(half * HALF, HALF)
        stacked = couple[:, rows, :].reshape(MODES * HALF, NO)
        for c in range(2):
            lefts = jnp.dot(stacked, slots[s, c], preferred_element_type=jnp.float32)
            lefts = lefts.astype(jnp.bfloat16)
            for a in range(MODES):
                prod[s, a, c, rows, :] = jnp.dot(
                    lefts[a * HALF:(a + 1) * HALF], couple[a], preferred_element_type=jnp.float32
                )

    def term(j, i, r):
        re = im = None
        for a in range(MODES):
            s = i + 1 - shift[a, j]
            p0 = prod[s, a, 0, pl.ds(r, STEP), :]
            p1 = prod[s, a, 1, pl.ds(r, STEP), :]
            d0 = weights[j, pl.ds(2 * a * NO + r, STEP), :].astype(jnp.float32)
            d1 = weights[j, pl.ds((2 * a + 1) * NO + r, STEP), :].astype(jnp.float32)
            one, two = p0 * d0 - p1 * d1, p0 * d1 + p1 * d0
            re = one if re is None else re + one
            im = two if im is None else im + two
        return re, im

    def over_rows(half, fn):
        def step(n, carry):
            fn(pl.multiple_of(half * HALF + n * STEP, STEP))
            return carry
        lax.fori_loop(0, HALF // STEP, step, 0)

    def sends(n, i, half):
        rows = pl.ds(half * HALF, HALF)
        a = pltpu.make_async_remote_copy(
            src_ref=to_left.at[i, :, rows, :], dst_ref=from_right.at[i, :, rows, :],
            send_sem=left_send.at[n], recv_sem=left_recv.at[n],
            device_id={"mom": left}, device_id_type=MESH)
        b = pltpu.make_async_remote_copy(
            src_ref=to_right.at[i, :, rows, :], dst_ref=from_left.at[i, :, rows, :],
            send_sem=right_send.at[n], recv_sem=right_recv.at[n],
            device_id={"mom": right}, device_id_type=MESH)
        return a, b

    have = set()
    copies = []
    for n, (i, half) in enumerate(CHUNKS):
        for s in (i + 1, i):
            if (s, half) in have:
                continue
            have.add((s, half))
            need("couple")
            if s > 0:
                need(s)
            elif half == 0:
                @pl.when(detour_over)
                def _():
                    out_of_way.wait_recv()
                    back.start()

                @pl.when(has_below)
                def _():
                    below.wait_recv()
            products(s, half)

        need("shift")
        need(("w", 0))
        need(("w", 2))

        def outer(r, i=i):
            re, im = term(0, i, r)
            to_left[i, 0, pl.ds(r, STEP), :] = re.astype(jnp.bfloat16)
            to_left[i, 1, pl.ds(r, STEP), :] = im.astype(jnp.bfloat16)
            re, im = term(2, i, r)
            to_right[i, 0, pl.ds(r, STEP), :] = re.astype(jnp.bfloat16)
            to_right[i, 1, pl.ds(r, STEP), :] = im.astype(jnp.bfloat16)

        over_rows(half, outer)

        need(("w", 1))

        def inner(r, i=i):
            re, im = term(1, i, r)
            own[i, 0, pl.ds(r, STEP), :] = re
            own[i, 1, pl.ds(r, STEP), :] = im

        if n > 0:
            over_rows(half, inner)
        else:
            pl.semaphore_wait(barrier, 2 + has_above.astype(jnp.int32) + detour_over.astype(jnp.int32))

            @pl.when(direct_up)
            def _():
                below.start()

            @pl.when(detour_up)
            def _():
                out_of_way.start()

            @pl.when(jnp.logical_not(has_below))
            def _():
                slots[0] = jnp.zeros((2, NO, NO), jnp.bfloat16)

        pair = sends(n, i, half)
        for copy in pair:
            copy.start()
        copies.append(pair)
        if n == 0:
            over_rows(half, inner)

    for n, (i, half) in enumerate(CHUNKS):
        for copy in copies[n]:
            copy.wait_recv()

        def final(r, i=i):
            for c in range(2):
                rows = pl.ds(r, STEP)
                total = own[i, c, rows, :] + from_right[i, c, rows, :].astype(jnp.float32)
                total = total + from_left[i, c, rows, :].astype(jnp.float32)
                out[i, c, rows, :] = total.astype(jnp.bfloat16)

        over_rows(half, final)

    for pair in copies:
        for copy in pair:
            copy.wait_send()

    @pl.when(direct_up)
    def _():
        below.wait_send()

    @pl.when(detour_up)
    def _():
        out_of_way.wait_send()

    @pl.when(detour_over)
    def _():
        back.wait_send()


def body(green, coupling, phonon, shift):
    block = (E_OUT, 2, NO, NO)
    n = len(CHUNKS)
    result = pl.pallas_call(
        kernel,
        out_shape=jax.ShapeDtypeStruct(block, jnp.bfloat16),
        in_specs=[pl.BlockSpec(memory_space=pltpu.HBM)] * 4,
        out_specs=pl.BlockSpec(memory_space=pltpu.VMEM),
        scratch_shapes=[
            pltpu.SMEM((MODES, NOFF), jnp.int32),
            pltpu.VMEM((E_OUT + 1, 2, NO, NO), jnp.bfloat16),
            pltpu.VMEM((MODES, NO, NO), jnp.bfloat16),
            pltpu.VMEM((NOFF, MODES * 2 * NO, NO), jnp.bfloat16),
            pltpu.VMEM((E_OUT + 1, MODES, 2, NO, NO), jnp.float32),
            pltpu.VMEM(block, jnp.bfloat16),
            pltpu.VMEM(block, jnp.bfloat16),
            pltpu.VMEM(block, jnp.bfloat16),
            pltpu.VMEM(block, jnp.bfloat16),
            pltpu.VMEM(block, jnp.float32),
            pltpu.VMEM((2, NO, NO), jnp.bfloat16),
            pltpu.SemaphoreType.DMA((E_OUT + 2 + NOFF,)),
            pltpu.SemaphoreType.DMA((2,)),
            pltpu.SemaphoreType.DMA((3,)),
            pltpu.SemaphoreType.DMA((n,)),
            pltpu.SemaphoreType.DMA((n,)),
            pltpu.SemaphoreType.DMA((n,)),
            pltpu.SemaphoreType.DMA((n,)),
        ],
        compiler_params=pltpu.CompilerParams(
            collective_id=0, has_side_effects=True, vmem_limit_bytes=VMEM_LIMIT
        ),
    )(
        pltpu.with_memory_space_constraint(green.reshape(block), pltpu.HBM),
        pltpu.with_memory_space_constraint(coupling, pltpu.HBM),
        pltpu.with_memory_space_constraint(phonon, pltpu.HBM),
        pltpu.with_memory_space_constraint(shift.T, pltpu.HBM),
    )
    return result.reshape((1, 1) + block)


def solution(mesh):
    placed = (P("mom", "energy", None, None, None, None), P(), P(), P())
    return jax.shard_map(
        body,
        mesh=mesh,
        in_specs=placed,
        out_specs=P("mom", "energy", None, None, None, None),
        check_vma=False,
    )
```

```python
import jax
import jax.numpy as jnp
from jax import lax
from jax.experimental import pallas as pl
from jax.experimental.pallas import tpu as pltpu
from jax.sharding import PartitionSpec as P

NO = 256
MODES = 2
E_OUT = 4
NOFF = 3
HALF = 128
STEP = 16
EDGE = 16
DETOUR = 3
VMEM_LIMIT = 24 * 1024 * 1024
MESH = pl.DeviceIdType.MESH

CHUNKS = [(1, 0), (1, 1), (2, 0), (2, 1), (3, 0), (3, 1), (0, 0), (0, 1)]


def kernel(
    green, coupling, phonon, shift_in, out,
    shift, slots, couple, weights, prod, to_left, to_right, from_right, from_left, own,
    relay, in_sem, below_sem, relay_sem, ready, left_send, left_recv, right_send, right_recv,
):
    me = lax.axis_index("mom")
    points = lax.axis_size("mom")
    group = lax.axis_index("energy")
    groups = lax.axis_size("energy")
    left = lax.rem(me + points - 1, points)
    right = lax.rem(me + 1, points)
    has_below = group > 0
    has_above = group < groups - 1

    detoured = (me == points // 2 - 1) | (me == points // 2)
    place = lax.rem(group, EDGE)
    detour_up = detoured & has_above & (place == EDGE - 1)
    detour_over = detoured & (group >= EDGE) & (place == DETOUR - 1)
    detour_down = detoured & has_below & (place == 0)
    direct_up = has_above & jnp.logical_not(detour_up)
    direct_down = has_below & jnp.logical_not(detour_down)
    over = lax.rem(group + DETOUR, groups)

    last = me == points - 1
    feeder = me == points - 2

    def tell(semaphore, device):
        pl.semaphore_signal(semaphore, inc=1, device_id=device, device_id_type=MESH)

    barrier = pltpu.get_barrier_semaphore()
    pl.semaphore_signal(barrier, inc=1, device_id={"mom": left}, device_id_type=MESH)

    @pl.when(jnp.logical_not(feeder))
    def _():
        pl.semaphore_signal(barrier, inc=1, device_id={"mom": right}, device_id_type=MESH)

    @pl.when(feeder & has_above)
    def _():
        pl.semaphore_signal(barrier, inc=1, device_id={"energy": group + 1}, device_id_type=MESH)

    @pl.when(direct_down & jnp.logical_not(last))
    def _():
        pl.semaphore_signal(barrier, inc=1, device_id={"energy": group - 1}, device_id_type=MESH)

    @pl.when(detour_over)
    def _():
        pl.semaphore_signal(barrier, inc=1, device_id={"energy": group - DETOUR}, device_id_type=MESH)

    @pl.when(detour_down)
    def _():
        pl.semaphore_signal(barrier, inc=1, device_id={"energy": group + DETOUR - 1}, device_id_type=MESH)

    loads = {"shift": pltpu.make_async_copy(shift_in, shift, in_sem.at[E_OUT + 1])}
    loads["couple"] = pltpu.make_async_copy(coupling, couple, in_sem.at[0])
    for s in range(E_OUT):
        loads[s + 1] = pltpu.make_async_copy(green.at[s], slots.at[s + 1], in_sem.at[s + 1])
    for j in range(NOFF):
        for half in range(2):
            rows = pl.ds(half * HALF, HALF)
            loads["w", j, half] = pltpu.make_async_copy(
                phonon.at[j, :, rows, :], weights.at[j, :, rows, :], in_sem.at[E_OUT + 2 + 2 * j + half])
    first = ["shift", "couple", 2, 1, ("w", 2, 0), ("w", 0, 0)]
    rest = [("w", 1, 0), 3, ("w", 2, 1), ("w", 0, 1), ("w", 1, 1), 4]
    for name in first:
        loads[name].start()
    waited = set()

    def need(name):
        if name not in waited:
            waited.add(name)
            loads[name].wait()

    below = pltpu.make_async_remote_copy(
        src_ref=green.at[E_OUT - 1],
        dst_ref=slots.at[0],
        send_sem=below_sem.at[0],
        recv_sem=below_sem.at[1],
        device_id={"energy": lax.rem(group + 1, groups)},
        device_id_type=MESH,
    )

    out_of_way = pltpu.make_async_remote_copy(
        src_ref=green.at[E_OUT - 1],
        dst_ref=relay,
        send_sem=relay_sem.at[0],
        recv_sem=relay_sem.at[1],
        device_id={"energy": over},
        device_id_type=MESH,
    )
    back = pltpu.make_async_remote_copy(
        src_ref=relay,
        dst_ref=slots.at[0],
        send_sem=relay_sem.at[2],
        recv_sem=below_sem.at[1],
        device_id={"energy": lax.rem(group + groups - DETOUR + 1, groups)},
        device_id_type=MESH,
    )

    def products(s, half):
        rows = pl.ds(half * HALF, HALF)
        stacked = couple[:, rows, :].reshape(MODES * HALF, NO)
        for c in range(2):
            lefts = jnp.dot(stacked, slots[s, c], preferred_element_type=jnp.float32)
            lefts = lefts.astype(jnp.bfloat16)
            for a in range(MODES):
                prod[s, a, c, rows, :] = jnp.dot(
                    lefts[a * HALF:(a + 1) * HALF], couple[a], preferred_element_type=jnp.float32
                )

    def term(j, i, r):
        re = im = None
        for a in range(MODES):
            s = i + 1 - shift[a, j]
            p0 = prod[s, a, 0, pl.ds(r, STEP), :]
            p1 = prod[s, a, 1, pl.ds(r, STEP), :]
            d0 = weights[j, 2 * a, pl.ds(r, STEP), :].astype(jnp.float32)
            d1 = weights[j, 2 * a + 1, pl.ds(r, STEP), :].astype(jnp.float32)
            one, two = p0 * d0 - p1 * d1, p0 * d1 + p1 * d0
            re = one if re is None else re + one
            im = two if im is None else im + two
        return re, im

    def over_rows(half, fn):
        def step(n, carry):
            fn(pl.multiple_of(half * HALF + n * STEP, STEP))
            return carry
        lax.fori_loop(0, HALF // STEP, step, 0)

    def sends(n, i, half):
        rows = pl.ds(half * HALF, HALF)
        a = pltpu.make_async_remote_copy(
            src_ref=to_left.at[i, :, rows, :], dst_ref=from_right.at[i, :, rows, :],
            send_sem=left_send.at[n], recv_sem=left_recv.at[n],
            device_id={"mom": left}, device_id_type=MESH)
        b = pltpu.make_async_remote_copy(
            src_ref=to_right.at[i, :, rows, :], dst_ref=from_left.at[i, :, rows, :],
            send_sem=right_send.at[n], recv_sem=right_recv.at[n],
            device_id={"mom": right}, device_id_type=MESH)
        return a, b

    have = set()
    copies = []
    for n, (i, half) in enumerate(CHUNKS):
        for s in (i + 1, i):
            if (s, half) in have:
                continue
            have.add((s, half))
            need("couple")
            if s > 0:
                need(s)
            elif half == 0:
                @pl.when(feeder & has_above)
                def _():
                    pl.semaphore_wait(ready.at[1], 1)
                    tell(ready.at[2], {"mom": right})

                @pl.when(last & has_above)
                def _():
                    pl.semaphore_wait(ready.at[2], 1)
                    below.start()

                @pl.when(detour_over)
                def _():
                    out_of_way.wait_recv()
                    back.start()

                @pl.when(has_below)
                def _():
                    below.wait_recv()
            products(s, half)

        need("shift")
        need(("w", 2, half))
        need(("w", 0, half))
        if n == 0:
            for name in rest:
                loads[name].start()

        def outer(r, i=i):
            re, im = term(0, i, r)
            to_left[i, 0, pl.ds(r, STEP), :] = re.astype(jnp.bfloat16)
            to_left[i, 1, pl.ds(r, STEP), :] = im.astype(jnp.bfloat16)
            re, im = term(2, i, r)
            to_right[i, 0, pl.ds(r, STEP), :] = re.astype(jnp.bfloat16)
            to_right[i, 1, pl.ds(r, STEP), :] = im.astype(jnp.bfloat16)

        over_rows(half, outer)

        def inner(r, i=i):
            re, im = term(1, i, r)
            own[i, 0, pl.ds(r, STEP), :] = re
            own[i, 1, pl.ds(r, STEP), :] = im

        to_the_left, to_the_right = sends(n, i, half)
        copies.append((to_the_left, to_the_right))
        if n > 0:
            need(("w", 1, half))
            over_rows(half, inner)
            to_the_right.start()
            if n == 1:
                @pl.when(last)
                def _():
                    pl.semaphore_wait(ready.at[0], 1)
                    copies[0][0].start()
            to_the_left.start()
        else:
            waits = 2 + has_above.astype(jnp.int32) + detour_over.astype(jnp.int32)
            waits = waits + (feeder & has_below).astype(jnp.int32)
            pl.semaphore_wait(barrier, jnp.where(last, 1, waits))
            to_the_right.start()

            @pl.when(jnp.logical_not(last))
            def _():
                to_the_left.start()

            @pl.when(feeder)
            def _():
                tell(ready.at[0], {"mom": right})

            @pl.when(feeder & has_below)
            def _():
                tell(ready.at[1], {"energy": group - 1})

            @pl.when(direct_up & jnp.logical_not(last))
            def _():
                below.start()

            @pl.when(detour_up)
            def _():
                out_of_way.start()

            @pl.when(jnp.logical_not(has_below))
            def _():
                slots[0] = jnp.zeros((2, NO, NO), jnp.bfloat16)

            need(("w", 1, half))
            over_rows(half, inner)

    for n, (i, half) in enumerate(CHUNKS):
        for copy in copies[n]:
            copy.wait_recv()

        def final(r, i=i):
            for c in range(2):
                rows = pl.ds(r, STEP)
                total = own[i, c, rows, :] + from_right[i, c, rows, :].astype(jnp.float32)
                total = total + from_left[i, c, rows, :].astype(jnp.float32)
                out[i, c, rows, :] = total.astype(jnp.bfloat16)

        over_rows(half, final)

    for pair in copies:
        for copy in pair:
            copy.wait_send()

    @pl.when(direct_up)
    def _():
        below.wait_send()

    @pl.when(detour_up)
    def _():
        out_of_way.wait_send()

    @pl.when(detour_over)
    def _():
        back.wait_send()


def body(green, coupling, phonon, shift):
    block = (E_OUT, 2, NO, NO)
    n = len(CHUNKS)
    result = pl.pallas_call(
        kernel,
        out_shape=jax.ShapeDtypeStruct(block, jnp.bfloat16),
        in_specs=[pl.BlockSpec(memory_space=pltpu.HBM)] * 4,
        out_specs=pl.BlockSpec(memory_space=pltpu.VMEM),
        scratch_shapes=[
            pltpu.SMEM((MODES, NOFF), jnp.int32),
            pltpu.VMEM((E_OUT + 1, 2, NO, NO), jnp.bfloat16),
            pltpu.VMEM((MODES, NO, NO), jnp.bfloat16),
            pltpu.VMEM((NOFF, MODES * 2, NO, NO), jnp.bfloat16),
            pltpu.VMEM((E_OUT + 1, MODES, 2, NO, NO), jnp.float32),
            pltpu.VMEM(block, jnp.bfloat16),
            pltpu.VMEM(block, jnp.bfloat16),
            pltpu.VMEM(block, jnp.bfloat16),
            pltpu.VMEM(block, jnp.bfloat16),
            pltpu.VMEM(block, jnp.float32),
            pltpu.VMEM((2, NO, NO), jnp.bfloat16),
            pltpu.SemaphoreType.DMA((E_OUT + 2 + 2 * NOFF,)),
            pltpu.SemaphoreType.DMA((2,)),
            pltpu.SemaphoreType.DMA((3,)),
            pltpu.SemaphoreType.REGULAR((3,)),
            pltpu.SemaphoreType.DMA((n,)),
            pltpu.SemaphoreType.DMA((n,)),
            pltpu.SemaphoreType.DMA((n,)),
            pltpu.SemaphoreType.DMA((n,)),
        ],
        compiler_params=pltpu.CompilerParams(
            collective_id=0, has_side_effects=True, vmem_limit_bytes=VMEM_LIMIT
        ),
    )(
        pltpu.with_memory_space_constraint(green.reshape(block), pltpu.HBM),
        pltpu.with_memory_space_constraint(coupling, pltpu.HBM),
        pltpu.with_memory_space_constraint(phonon.reshape(NOFF, MODES * 2, NO, NO), pltpu.HBM),
        pltpu.with_memory_space_constraint(shift.T, pltpu.HBM),
    )
    return result.reshape((1, 1) + block)


def solution(mesh):
    placed = (P("mom", "energy", None, None, None, None), P(), P(), P())
    return jax.shard_map(
        body,
        mesh=mesh,
        in_specs=placed,
        out_specs=P("mom", "energy", None, None, None, None),
        check_vma=False,
    )
```

```python
import functools

import jax
import jax.numpy as jnp
from jax import lax
from jax.experimental import pallas as pl
from jax.experimental.pallas import tpu as pltpu
from jax.sharding import PartitionSpec as P

NO = 256
MODES = 2
E_OUT = 4
NOFF = 3
HALF = 128
STEP = 16
EDGE = 16
DETOUR = 3
GAP = 32
VMEM_LIMIT = 24 * 1024 * 1024
MESH = pl.DeviceIdType.MESH

CHUNKS = [(1, 0), (1, 1), (2, 0), (2, 1), (3, 0), (3, 1), (0, 0), (0, 1)]


def kernel(
    green, coupling, phonon, shift_in, out,
    shift, slots, couple, weights, prod, to_left, to_right, from_right, from_left, own,
    relay, in_sem, below_sem, relay_sem, ready, left_send, left_recv, right_send, right_recv,
):
    loads = {"shift": pltpu.make_async_copy(shift_in, shift, in_sem.at[E_OUT + 1])}
    loads["couple"] = pltpu.make_async_copy(coupling, couple, in_sem.at[0])
    for s in range(E_OUT):
        loads[s + 1] = pltpu.make_async_copy(green.at[s], slots.at[s + 1], in_sem.at[s + 1])
    for j in range(NOFF):
        for half in range(2):
            rows = pl.ds(half * HALF, HALF)
            loads["w", j, half] = pltpu.make_async_copy(
                phonon.at[j, :, rows, :], weights.at[j, :, rows, :], in_sem.at[E_OUT + 2 + 2 * j + half])
    first = ["shift", "couple", 2, 1, ("w", 2, 0), ("w", 0, 0)]
    rest = [("w", 1, 0), 3, ("w", 2, 1), ("w", 0, 1), ("w", 1, 1), 4]
    for name in first:
        loads[name].start()
    me = lax.axis_index("mom")
    points = lax.axis_size("mom")
    group = lax.axis_index("energy")
    groups = lax.axis_size("energy")
    left = lax.rem(me + points - 1, points)
    right = lax.rem(me + 1, points)
    has_below = group > 0
    has_above = group < groups - 1

    detoured = (me == points // 2 - 1) | (me == points // 2)
    place = lax.rem(group, EDGE)
    detour_up = detoured & has_above & (place == EDGE - 1)
    detour_over = detoured & (group >= EDGE) & (place == DETOUR - 1)
    detour_down = detoured & has_below & (place == 0)
    direct_up = has_above & jnp.logical_not(detour_up)
    direct_down = has_below & jnp.logical_not(detour_down)
    over = lax.rem(group + DETOUR, groups)

    last = me == points - 1
    feeder = me == points - 2

    def tell(semaphore, device):
        pl.semaphore_signal(semaphore, inc=1, device_id=device, device_id_type=MESH)

    barrier = pltpu.get_barrier_semaphore()
    pl.semaphore_signal(barrier, inc=1, device_id={"mom": left}, device_id_type=MESH)

    @pl.when(jnp.logical_not(feeder))
    def _():
        pl.semaphore_signal(barrier, inc=1, device_id={"mom": right}, device_id_type=MESH)

    @pl.when(feeder & has_above)
    def _():
        pl.semaphore_signal(barrier, inc=1, device_id={"energy": group + 1}, device_id_type=MESH)

    @pl.when(direct_down & jnp.logical_not(last))
    def _():
        pl.semaphore_signal(barrier, inc=1, device_id={"energy": group - 1}, device_id_type=MESH)

    @pl.when(detour_over)
    def _():
        pl.semaphore_signal(barrier, inc=1, device_id={"energy": group - DETOUR}, device_id_type=MESH)

    @pl.when(detour_down)
    def _():
        pl.semaphore_signal(barrier, inc=1, device_id={"energy": group + DETOUR - 1}, device_id_type=MESH)

    waited = set()

    def need(name):
        if name not in waited:
            waited.add(name)
            loads[name].wait()

    below = pltpu.make_async_remote_copy(
        src_ref=green.at[E_OUT - 1],
        dst_ref=slots.at[0],
        send_sem=below_sem.at[0],
        recv_sem=below_sem.at[1],
        device_id={"energy": lax.rem(group + 1, groups)},
        device_id_type=MESH,
    )

    out_of_way = pltpu.make_async_remote_copy(
        src_ref=green.at[E_OUT - 1],
        dst_ref=relay,
        send_sem=relay_sem.at[0],
        recv_sem=relay_sem.at[1],
        device_id={"energy": over},
        device_id_type=MESH,
    )
    back = pltpu.make_async_remote_copy(
        src_ref=relay,
        dst_ref=slots.at[0],
        send_sem=relay_sem.at[2],
        recv_sem=below_sem.at[1],
        device_id={"energy": lax.rem(group + groups - DETOUR + 1, groups)},
        device_id_type=MESH,
    )

    def products(s, half):
        rows = pl.ds(half * HALF, HALF)
        stacked = couple[:, rows, :].reshape(MODES * HALF, NO)
        for c in range(2):
            lefts = jnp.dot(stacked, slots[s, c], preferred_element_type=jnp.float32)
            lefts = lefts.astype(jnp.bfloat16)
            for a in range(MODES):
                prod[s, a, c, rows, :] = jnp.dot(
                    lefts[a * HALF:(a + 1) * HALF], couple[a], preferred_element_type=jnp.float32
                )

    def term(j, i, r):
        re = im = None
        for a in range(MODES):
            s = i + 1 - shift[a, j]
            p0 = prod[s, a, 0, pl.ds(r, STEP), :]
            p1 = prod[s, a, 1, pl.ds(r, STEP), :]
            d0 = weights[j, 2 * a, pl.ds(r, STEP), :].astype(jnp.float32)
            d1 = weights[j, 2 * a + 1, pl.ds(r, STEP), :].astype(jnp.float32)
            one, two = p0 * d0 - p1 * d1, p0 * d1 + p1 * d0
            re = one if re is None else re + one
            im = two if im is None else im + two
        return re, im

    def over_rows(half, fn, begin=0, end=HALF):
        def step(n, carry):
            fn(pl.multiple_of(half * HALF + n * STEP, STEP))
            return carry
        lax.fori_loop(begin // STEP, end // STEP, step, 0)

    def sends(n, i, half):
        rows = pl.ds(half * HALF, HALF)
        a = pltpu.make_async_remote_copy(
            src_ref=to_left.at[i, :, rows, :], dst_ref=from_right.at[i, :, rows, :],
            send_sem=left_send.at[n], recv_sem=left_recv.at[n],
            device_id={"mom": left}, device_id_type=MESH)
        b = pltpu.make_async_remote_copy(
            src_ref=to_right.at[i, :, rows, :], dst_ref=from_left.at[i, :, rows, :],
            send_sem=right_send.at[n], recv_sem=right_recv.at[n],
            device_id={"mom": right}, device_id_type=MESH)
        return a, b

    def inner(r, i):
        re, im = term(1, i, r)
        own[i, 0, pl.ds(r, STEP), :] = re
        own[i, 1, pl.ds(r, STEP), :] = im

    have = set()
    copies = []
    for n, (i, half) in enumerate(CHUNKS):
        for s in (i + 1, i):
            if (s, half) in have:
                continue
            have.add((s, half))
            need("couple")
            if s > 0:
                need(s)
            elif half == 0:
                @pl.when(feeder & has_above)
                def _():
                    pl.semaphore_wait(ready.at[1], 1)
                    tell(ready.at[2], {"mom": right})

                @pl.when(last & has_above)
                def _():
                    pl.semaphore_wait(ready.at[2], 1)
                    below.start()

                @pl.when(detour_over)
                def _():
                    out_of_way.wait_recv()
                    back.start()

                @pl.when(has_below)
                def _():
                    below.wait_recv()
            products(s, half)

        need("shift")
        need(("w", 2, half))
        need(("w", 0, half))
        if n == 0:
            for name in rest:
                loads[name].start()

        def outer(r, i=i):
            re, im = term(0, i, r)
            to_left[i, 0, pl.ds(r, STEP), :] = re.astype(jnp.bfloat16)
            to_left[i, 1, pl.ds(r, STEP), :] = im.astype(jnp.bfloat16)
            re, im = term(2, i, r)
            to_right[i, 0, pl.ds(r, STEP), :] = re.astype(jnp.bfloat16)
            to_right[i, 1, pl.ds(r, STEP), :] = im.astype(jnp.bfloat16)

        over_rows(half, outer)

        to_the_left, to_the_right = sends(n, i, half)
        copies.append((to_the_left, to_the_right))
        if n > 0:
            for h in {0, half}:
                need(("w", 1, h))
            over_rows(half, functools.partial(inner, i=i), 0, GAP)
            to_the_right.start()
            if n == 1:
                @pl.when(last)
                def _():
                    pl.semaphore_wait(ready.at[0], 1)
                    copies[0][0].start()
            to_the_left.start()
        else:
            waits = 2 + has_above.astype(jnp.int32) + detour_over.astype(jnp.int32)
            waits = waits + (feeder & has_below).astype(jnp.int32)
            pl.semaphore_wait(barrier, jnp.where(last, 1, waits))
            to_the_right.start()

            @pl.when(jnp.logical_not(last))
            def _():
                to_the_left.start()

            @pl.when(feeder)
            def _():
                tell(ready.at[0], {"mom": right})

            @pl.when(feeder & has_below)
            def _():
                tell(ready.at[1], {"energy": group - 1})

            @pl.when(direct_up & jnp.logical_not(last))
            def _():
                below.start()

            @pl.when(detour_up)
            def _():
                out_of_way.start()

            @pl.when(jnp.logical_not(has_below))
            def _():
                slots[0] = jnp.zeros((2, NO, NO), jnp.bfloat16)


    for n, (i, half) in enumerate(CHUNKS):
        over_rows(half, functools.partial(inner, i=i), GAP if n > 0 else 0)

    for n, (i, half) in enumerate(CHUNKS):
        for copy in copies[n]:
            copy.wait_recv()

        def final(r, i=i):
            for c in range(2):
                rows = pl.ds(r, STEP)
                total = own[i, c, rows, :] + from_right[i, c, rows, :].astype(jnp.float32)
                total = total + from_left[i, c, rows, :].astype(jnp.float32)
                out[i, c, rows, :] = total.astype(jnp.bfloat16)

        over_rows(half, final)

    for pair in copies:
        for copy in pair:
            copy.wait_send()

    @pl.when(direct_up)
    def _():
        below.wait_send()

    @pl.when(detour_up)
    def _():
        out_of_way.wait_send()

    @pl.when(detour_over)
    def _():
        back.wait_send()


def body(green, coupling, phonon, shift):
    block = (E_OUT, 2, NO, NO)
    n = len(CHUNKS)
    result = pl.pallas_call(
        kernel,
        out_shape=jax.ShapeDtypeStruct(block, jnp.bfloat16),
        in_specs=[pl.BlockSpec(memory_space=pltpu.HBM)] * 4,
        out_specs=pl.BlockSpec(memory_space=pltpu.VMEM),
        scratch_shapes=[
            pltpu.SMEM((MODES, NOFF), jnp.int32),
            pltpu.VMEM((E_OUT + 1, 2, NO, NO), jnp.bfloat16),
            pltpu.VMEM((MODES, NO, NO), jnp.bfloat16),
            pltpu.VMEM((NOFF, MODES * 2, NO, NO), jnp.bfloat16),
            pltpu.VMEM((E_OUT + 1, MODES, 2, NO, NO), jnp.float32),
            pltpu.VMEM(block, jnp.bfloat16),
            pltpu.VMEM(block, jnp.bfloat16),
            pltpu.VMEM(block, jnp.bfloat16),
            pltpu.VMEM(block, jnp.bfloat16),
            pltpu.VMEM(block, jnp.float32),
            pltpu.VMEM((2, NO, NO), jnp.bfloat16),
            pltpu.SemaphoreType.DMA((E_OUT + 2 + 2 * NOFF,)),
            pltpu.SemaphoreType.DMA((2,)),
            pltpu.SemaphoreType.DMA((3,)),
            pltpu.SemaphoreType.REGULAR((3,)),
            pltpu.SemaphoreType.DMA((n,)),
            pltpu.SemaphoreType.DMA((n,)),
            pltpu.SemaphoreType.DMA((n,)),
            pltpu.SemaphoreType.DMA((n,)),
        ],
        compiler_params=pltpu.CompilerParams(
            collective_id=0, has_side_effects=True, vmem_limit_bytes=VMEM_LIMIT
        ),
    )(
        pltpu.with_memory_space_constraint(green.reshape(block), pltpu.HBM),
        pltpu.with_memory_space_constraint(coupling, pltpu.HBM),
        pltpu.with_memory_space_constraint(phonon.reshape(NOFF, MODES * 2, NO, NO), pltpu.HBM),
        pltpu.with_memory_space_constraint(shift.T, pltpu.HBM),
    )
    return result.reshape((1, 1) + block)


def solution(mesh):
    placed = (P("mom", "energy", None, None, None, None), P(), P(), P())
    return jax.shard_map(
        body,
        mesh=mesh,
        in_specs=placed,
        out_specs=P("mom", "energy", None, None, None, None),
        check_vma=False,
    )
```

```python
import functools

import jax
import jax.numpy as jnp
from jax import lax
from jax.experimental import pallas as pl
from jax.experimental.pallas import tpu as pltpu
from jax.sharding import PartitionSpec as P

NO = 256
MODES = 2
E_OUT = 4
NOFF = 3
HALF = 128
STEP = 16
EDGE = 16
DETOUR = 3
GAP = 32
VMEM_LIMIT = 24 * 1024 * 1024
MESH = pl.DeviceIdType.MESH

CHUNKS = [(1, 0), (1, 1), (2, 0), (2, 1), (3, 0), (3, 1), (0, 0), (0, 1)]


def kernel(
    green, coupling, phonon, shift_in, out,
    shift, slots, couple, weights, prod, to_left, to_right, from_right, from_left, own,
    relay, in_sem, below_sem, relay_sem, ready, left_send, left_recv, right_send, right_recv,
):
    loads = {"shift": pltpu.make_async_copy(shift_in, shift, in_sem.at[E_OUT + 1])}
    loads["couple"] = pltpu.make_async_copy(coupling, couple, in_sem.at[0])
    for s in range(E_OUT):
        loads[s + 1] = pltpu.make_async_copy(green.at[s], slots.at[s + 1], in_sem.at[s + 1])
    for j in range(NOFF):
        for half in range(2):
            rows = pl.ds(half * HALF, HALF)
            loads["w", j, half] = pltpu.make_async_copy(
                phonon.at[j, :, rows, :], weights.at[j, :, rows, :], in_sem.at[E_OUT + 2 + 2 * j + half])
    first = ["shift", "couple", 2, 1, ("w", 2, 0), ("w", 0, 0)]
    rest = [("w", 1, 0), 3, ("w", 2, 1), ("w", 0, 1), ("w", 1, 1), 4]
    for name in first:
        loads[name].start()
    me = lax.axis_index("mom")
    points = lax.axis_size("mom")
    group = lax.axis_index("energy")
    groups = lax.axis_size("energy")
    left = lax.rem(me + points - 1, points)
    right = lax.rem(me + 1, points)
    has_below = group > 0
    has_above = group < groups - 1

    detoured = (me == points // 2 - 1) | (me == points // 2)
    place = lax.rem(group, EDGE)
    detour_up = detoured & has_above & (place == EDGE - 1)
    detour_over = detoured & (group >= EDGE) & (place == DETOUR - 1)
    detour_down = detoured & has_below & (place == 0)
    direct_up = has_above & jnp.logical_not(detour_up)
    direct_down = has_below & jnp.logical_not(detour_down)
    over = lax.rem(group + DETOUR, groups)

    last = me == points - 1
    feeder = me == points - 2

    def tell(semaphore, device):
        pl.semaphore_signal(semaphore, inc=1, device_id=device, device_id_type=MESH)

    barrier = pltpu.get_barrier_semaphore()
    pl.semaphore_signal(barrier, inc=1, device_id={"mom": left}, device_id_type=MESH)

    @pl.when(jnp.logical_not(feeder))
    def _():
        pl.semaphore_signal(barrier, inc=1, device_id={"mom": right}, device_id_type=MESH)

    @pl.when(feeder & has_above)
    def _():
        pl.semaphore_signal(barrier, inc=1, device_id={"energy": group + 1}, device_id_type=MESH)

    @pl.when(direct_down & jnp.logical_not(last))
    def _():
        pl.semaphore_signal(barrier, inc=1, device_id={"energy": group - 1}, device_id_type=MESH)

    @pl.when(detour_over)
    def _():
        pl.semaphore_signal(barrier, inc=1, device_id={"energy": group - DETOUR}, device_id_type=MESH)

    @pl.when(detour_down)
    def _():
        pl.semaphore_signal(barrier, inc=1, device_id={"energy": group + DETOUR - 1}, device_id_type=MESH)

    waited = set()

    def need(name):
        if name not in waited:
            waited.add(name)
            loads[name].wait()

    below = pltpu.make_async_remote_copy(
        src_ref=green.at[E_OUT - 1],
        dst_ref=slots.at[0],
        send_sem=below_sem.at[0],
        recv_sem=below_sem.at[1],
        device_id={"energy": lax.rem(group + 1, groups)},
        device_id_type=MESH,
    )

    out_of_way = pltpu.make_async_remote_copy(
        src_ref=green.at[E_OUT - 1],
        dst_ref=relay,
        send_sem=relay_sem.at[0],
        recv_sem=relay_sem.at[1],
        device_id={"energy": over},
        device_id_type=MESH,
    )
    back = pltpu.make_async_remote_copy(
        src_ref=relay,
        dst_ref=slots.at[0],
        send_sem=relay_sem.at[2],
        recv_sem=below_sem.at[1],
        device_id={"energy": lax.rem(group + groups - DETOUR + 1, groups)},
        device_id_type=MESH,
    )

    def products(s, half):
        rows = pl.ds(half * HALF, HALF)
        stacked = couple[:, rows, :].reshape(MODES * HALF, NO)
        for c in range(2):
            lefts = jnp.dot(stacked, slots[s, c], preferred_element_type=jnp.float32)
            lefts = lefts.astype(jnp.bfloat16)
            for a in range(MODES):
                prod[s, a, c, rows, :] = jnp.dot(
                    lefts[a * HALF:(a + 1) * HALF], couple[a], preferred_element_type=jnp.float32
                )

    def term(j, i, r):
        re = im = None
        for a in range(MODES):
            s = i + 1 - shift[a, j]
            p0 = prod[s, a, 0, pl.ds(r, STEP), :]
            p1 = prod[s, a, 1, pl.ds(r, STEP), :]
            d0 = weights[j, 2 * a, pl.ds(r, STEP), :].astype(jnp.float32)
            d1 = weights[j, 2 * a + 1, pl.ds(r, STEP), :].astype(jnp.float32)
            one, two = p0 * d0 - p1 * d1, p0 * d1 + p1 * d0
            re = one if re is None else re + one
            im = two if im is None else im + two
        return re, im

    def over_rows(half, fn, begin=0, end=HALF):
        def step(n, carry):
            fn(pl.multiple_of(half * HALF + n * STEP, STEP))
            return carry
        lax.fori_loop(begin // STEP, end // STEP, step, 0)

    def sends(n, i, half):
        rows = pl.ds(half * HALF, HALF)
        a = pltpu.make_async_remote_copy(
            src_ref=to_left.at[i, :, rows, :], dst_ref=from_right.at[i, :, rows, :],
            send_sem=left_send.at[n], recv_sem=left_recv.at[n],
            device_id={"mom": left}, device_id_type=MESH)
        b = pltpu.make_async_remote_copy(
            src_ref=to_right.at[i, :, rows, :], dst_ref=from_left.at[i, :, rows, :],
            send_sem=right_send.at[n], recv_sem=right_recv.at[n],
            device_id={"mom": right}, device_id_type=MESH)
        return a, b

    def inner(r, i):
        re, im = term(1, i, r)
        own[i, 0, pl.ds(r, STEP), :] = re
        own[i, 1, pl.ds(r, STEP), :] = im

    def weigh(r, j, i, target):
        re, im = term(j, i, r)
        target[i, 0, pl.ds(r, STEP), :] = re.astype(jnp.bfloat16)
        target[i, 1, pl.ds(r, STEP), :] = im.astype(jnp.bfloat16)

    have = set()
    copies = []
    for n, (i, half) in enumerate(CHUNKS):
        for s in (i + 1, i):
            if (s, half) in have:
                continue
            have.add((s, half))
            need("couple")
            if s > 0:
                need(s)
            elif half == 0:
                @pl.when(feeder & has_above)
                def _():
                    pl.semaphore_wait(ready.at[1], 1)
                    tell(ready.at[2], {"mom": right})

                @pl.when(last & has_above)
                def _():
                    pl.semaphore_wait(ready.at[2], 1)
                    below.start()

                @pl.when(detour_over)
                def _():
                    out_of_way.wait_recv()
                    back.start()

                @pl.when(has_below)
                def _():
                    below.wait_recv()
            products(s, half)

        need("shift")
        need(("w", 2, half))
        need(("w", 0, half))
        if n == 0:
            for name in rest:
                loads[name].start()

        over_rows(half, functools.partial(weigh, j=2, i=i, target=to_right))
        go_left = functools.partial(weigh, j=0, i=i, target=to_left)
        over_rows(half, go_left, 0, GAP)
        to_the_left, to_the_right = sends(n, i, half)
        copies.append((to_the_left, to_the_right))
        if n > 0:
            need(("w", 1, half))
            to_the_right.start()
            over_rows(half, go_left, GAP)
            over_rows(half, functools.partial(inner, i=i), 0, GAP)
            if n == 1:
                @pl.when(last)
                def _():
                    pl.semaphore_wait(ready.at[0], 1)
                    copies[0][0].start()
            to_the_left.start()
        else:
            waits = 2 + has_above.astype(jnp.int32) + detour_over.astype(jnp.int32)
            waits = waits + (feeder & has_below).astype(jnp.int32)
            pl.semaphore_wait(barrier, jnp.where(last, 1, waits))
            to_the_right.start()
            over_rows(half, go_left, GAP)
            need(("w", 1, half))
            over_rows(half, functools.partial(inner, i=i), 0, GAP)

            @pl.when(jnp.logical_not(last))
            def _():
                to_the_left.start()

            @pl.when(feeder)
            def _():
                tell(ready.at[0], {"mom": right})

            @pl.when(feeder & has_below)
            def _():
                tell(ready.at[1], {"energy": group - 1})

            @pl.when(direct_up & jnp.logical_not(last))
            def _():
                below.start()

            @pl.when(detour_up)
            def _():
                out_of_way.start()

            @pl.when(jnp.logical_not(has_below))
            def _():
                slots[0] = jnp.zeros((2, NO, NO), jnp.bfloat16)


    for n, (i, half) in enumerate(CHUNKS):
        over_rows(half, functools.partial(inner, i=i), GAP)

    for n, (i, half) in enumerate(CHUNKS):
        for copy in copies[n]:
            copy.wait_recv()

        def final(r, i=i):
            for c in range(2):
                rows = pl.ds(r, STEP)
                total = own[i, c, rows, :] + from_right[i, c, rows, :].astype(jnp.float32)
                total = total + from_left[i, c, rows, :].astype(jnp.float32)
                out[i, c, rows, :] = total.astype(jnp.bfloat16)

        over_rows(half, final)

    for pair in copies:
        for copy in pair:
            copy.wait_send()

    @pl.when(direct_up)
    def _():
        below.wait_send()

    @pl.when(detour_up)
    def _():
        out_of_way.wait_send()

    @pl.when(detour_over)
    def _():
        back.wait_send()


def body(green, coupling, phonon, shift):
    block = (E_OUT, 2, NO, NO)
    n = len(CHUNKS)
    result = pl.pallas_call(
        kernel,
        out_shape=jax.ShapeDtypeStruct(block, jnp.bfloat16),
        in_specs=[pl.BlockSpec(memory_space=pltpu.HBM)] * 4,
        out_specs=pl.BlockSpec(memory_space=pltpu.VMEM),
        scratch_shapes=[
            pltpu.SMEM((MODES, NOFF), jnp.int32),
            pltpu.VMEM((E_OUT + 1, 2, NO, NO), jnp.bfloat16),
            pltpu.VMEM((MODES, NO, NO), jnp.bfloat16),
            pltpu.VMEM((NOFF, MODES * 2, NO, NO), jnp.bfloat16),
            pltpu.VMEM((E_OUT + 1, MODES, 2, NO, NO), jnp.float32),
            pltpu.VMEM(block, jnp.bfloat16),
            pltpu.VMEM(block, jnp.bfloat16),
            pltpu.VMEM(block, jnp.bfloat16),
            pltpu.VMEM(block, jnp.bfloat16),
            pltpu.VMEM(block, jnp.float32),
            pltpu.VMEM((2, NO, NO), jnp.bfloat16),
            pltpu.SemaphoreType.DMA((E_OUT + 2 + 2 * NOFF,)),
            pltpu.SemaphoreType.DMA((2,)),
            pltpu.SemaphoreType.DMA((3,)),
            pltpu.SemaphoreType.REGULAR((3,)),
            pltpu.SemaphoreType.DMA((n,)),
            pltpu.SemaphoreType.DMA((n,)),
            pltpu.SemaphoreType.DMA((n,)),
            pltpu.SemaphoreType.DMA((n,)),
        ],
        compiler_params=pltpu.CompilerParams(
            collective_id=0, has_side_effects=True, vmem_limit_bytes=VMEM_LIMIT
        ),
    )(
        pltpu.with_memory_space_constraint(green.reshape(block), pltpu.HBM),
        pltpu.with_memory_space_constraint(coupling, pltpu.HBM),
        pltpu.with_memory_space_constraint(phonon.reshape(NOFF, MODES * 2, NO, NO), pltpu.HBM),
        pltpu.with_memory_space_constraint(shift.T, pltpu.HBM),
    )
    return result.reshape((1, 1) + block)


def solution(mesh):
    placed = (P("mom", "energy", None, None, None, None), P(), P(), P())
    return jax.shard_map(
        body,
        mesh=mesh,
        in_specs=placed,
        out_specs=P("mom", "energy", None, None, None, None),
        check_vma=False,
    )
```

```python
import functools

import jax
import jax.numpy as jnp
from jax import lax
from jax.experimental import pallas as pl
from jax.experimental.pallas import tpu as pltpu
from jax.sharding import PartitionSpec as P

NO = 256
MODES = 2
E_OUT = 4
NOFF = 3
HALF = 128
STEP = 16
EDGE = 16
DETOUR = 3
GAP = 16
VMEM_LIMIT = 24 * 1024 * 1024
MESH = pl.DeviceIdType.MESH

CHUNKS = [(1, 0), (1, 1), (2, 0), (2, 1), (3, 0), (3, 1), (0, 0), (0, 1)]


def kernel(
    green, coupling, phonon, shift_in, out,
    shift, slots, couple, weights, prod, to_left, to_right, from_right, from_left, own,
    relay, in_sem, below_sem, relay_sem, ready, left_send, left_recv, right_send, right_recv,
):
    loads = {"shift": pltpu.make_async_copy(shift_in, shift, in_sem.at[E_OUT + 1])}
    loads["couple"] = pltpu.make_async_copy(coupling, couple, in_sem.at[0])
    for s in range(E_OUT):
        loads[s + 1] = pltpu.make_async_copy(green.at[s], slots.at[s + 1], in_sem.at[s + 1])
    for j in range(NOFF):
        for half in range(2):
            rows = pl.ds(half * HALF, HALF)
            loads["w", j, half] = pltpu.make_async_copy(
                phonon.at[j, :, rows, :], weights.at[j, :, rows, :], in_sem.at[E_OUT + 2 + 2 * j + half])
    first = ["shift", "couple", 2, 1, ("w", 2, 0), ("w", 0, 0)]
    rest = [("w", 1, 0), 3, ("w", 2, 1), ("w", 0, 1), ("w", 1, 1), 4]
    for name in first:
        loads[name].start()
    me = lax.axis_index("mom")
    points = lax.axis_size("mom")
    group = lax.axis_index("energy")
    groups = lax.axis_size("energy")
    left = lax.rem(me + points - 1, points)
    right = lax.rem(me + 1, points)
    has_below = group > 0
    has_above = group < groups - 1

    detoured = (me == points // 2 - 1) | (me == points // 2)
    place = lax.rem(group, EDGE)
    detour_up = detoured & has_above & (place == EDGE - 1)
    detour_over = detoured & (group >= EDGE) & (place == DETOUR - 1)
    detour_down = detoured & has_below & (place == 0)
    direct_up = has_above & jnp.logical_not(detour_up)
    direct_down = has_below & jnp.logical_not(detour_down)
    over = lax.rem(group + DETOUR, groups)

    last = me == points - 1
    feeder = me == points - 2

    def tell(semaphore, device):
        pl.semaphore_signal(semaphore, inc=1, device_id=device, device_id_type=MESH)

    barrier = pltpu.get_barrier_semaphore()
    pl.semaphore_signal(barrier, inc=1, device_id={"mom": left}, device_id_type=MESH)

    @pl.when(jnp.logical_not(feeder))
    def _():
        pl.semaphore_signal(barrier, inc=1, device_id={"mom": right}, device_id_type=MESH)

    @pl.when(feeder & has_above)
    def _():
        pl.semaphore_signal(barrier, inc=1, device_id={"energy": group + 1}, device_id_type=MESH)

    @pl.when(direct_down & jnp.logical_not(last))
    def _():
        pl.semaphore_signal(barrier, inc=1, device_id={"energy": group - 1}, device_id_type=MESH)

    @pl.when(detour_over)
    def _():
        pl.semaphore_signal(barrier, inc=1, device_id={"energy": group - DETOUR}, device_id_type=MESH)

    @pl.when(detour_down)
    def _():
        pl.semaphore_signal(barrier, inc=1, device_id={"energy": group + DETOUR - 1}, device_id_type=MESH)

    waited = set()

    def need(name):
        if name not in waited:
            waited.add(name)
            loads[name].wait()

    below = pltpu.make_async_remote_copy(
        src_ref=green.at[E_OUT - 1],
        dst_ref=slots.at[0],
        send_sem=below_sem.at[0],
        recv_sem=below_sem.at[1],
        device_id={"energy": lax.rem(group + 1, groups)},
        device_id_type=MESH,
    )

    out_of_way = pltpu.make_async_remote_copy(
        src_ref=green.at[E_OUT - 1],
        dst_ref=relay,
        send_sem=relay_sem.at[0],
        recv_sem=relay_sem.at[1],
        device_id={"energy": over},
        device_id_type=MESH,
    )
    back = pltpu.make_async_remote_copy(
        src_ref=relay,
        dst_ref=slots.at[0],
        send_sem=relay_sem.at[2],
        recv_sem=below_sem.at[1],
        device_id={"energy": lax.rem(group + groups - DETOUR + 1, groups)},
        device_id_type=MESH,
    )

    def products(s, half):
        rows = pl.ds(half * HALF, HALF)
        stacked = couple[:, rows, :].reshape(MODES * HALF, NO)
        for c in range(2):
            lefts = jnp.dot(stacked, slots[s, c], preferred_element_type=jnp.float32)
            lefts = lefts.astype(jnp.bfloat16)
            for a in range(MODES):
                prod[s, a, c, rows, :] = jnp.dot(
                    lefts[a * HALF:(a + 1) * HALF], couple[a], preferred_element_type=jnp.float32
                )

    def term(j, i, r):
        re = im = None
        for a in range(MODES):
            s = i + 1 - shift[a, j]
            p0 = prod[s, a, 0, pl.ds(r, STEP), :]
            p1 = prod[s, a, 1, pl.ds(r, STEP), :]
            d0 = weights[j, 2 * a, pl.ds(r, STEP), :].astype(jnp.float32)
            d1 = weights[j, 2 * a + 1, pl.ds(r, STEP), :].astype(jnp.float32)
            one, two = p0 * d0 - p1 * d1, p0 * d1 + p1 * d0
            re = one if re is None else re + one
            im = two if im is None else im + two
        return re, im

    def over_rows(half, fn, begin=0, end=HALF):
        def step(n, carry):
            fn(pl.multiple_of(half * HALF + n * STEP, STEP))
            return carry
        lax.fori_loop(begin // STEP, end // STEP, step, 0)

    def sends(n, i, half):
        rows = pl.ds(half * HALF, HALF)
        a = pltpu.make_async_remote_copy(
            src_ref=to_left.at[i, :, rows, :], dst_ref=from_right.at[i, :, rows, :],
            send_sem=left_send.at[n], recv_sem=left_recv.at[n],
            device_id={"mom": left}, device_id_type=MESH)
        b = pltpu.make_async_remote_copy(
            src_ref=to_right.at[i, :, rows, :], dst_ref=from_left.at[i, :, rows, :],
            send_sem=right_send.at[n], recv_sem=right_recv.at[n],
            device_id={"mom": right}, device_id_type=MESH)
        return a, b

    def inner(r, i):
        re, im = term(1, i, r)
        own[i, 0, pl.ds(r, STEP), :] = re
        own[i, 1, pl.ds(r, STEP), :] = im

    def weigh(r, j, i, target):
        re, im = term(j, i, r)
        target[i, 0, pl.ds(r, STEP), :] = re.astype(jnp.bfloat16)
        target[i, 1, pl.ds(r, STEP), :] = im.astype(jnp.bfloat16)

    have = set()
    copies = []
    for n, (i, half) in enumerate(CHUNKS):
        for s in (i + 1, i):
            if (s, half) in have:
                continue
            have.add((s, half))
            need("couple")
            if s > 0:
                need(s)
            elif half == 0:
                @pl.when(feeder & has_above)
                def _():
                    pl.semaphore_wait(ready.at[1], 1)
                    tell(ready.at[2], {"mom": right})

                @pl.when(last & has_above)
                def _():
                    pl.semaphore_wait(ready.at[2], 1)
                    below.start()

                @pl.when(detour_over)
                def _():
                    out_of_way.wait_recv()
                    back.start()

                @pl.when(has_below)
                def _():
                    below.wait_recv()
            products(s, half)

        need("shift")
        need(("w", 2, half))
        need(("w", 0, half))
        if n == 0:
            for name in rest:
                loads[name].start()

        over_rows(half, functools.partial(weigh, j=2, i=i, target=to_right))
        go_left = functools.partial(weigh, j=0, i=i, target=to_left)
        over_rows(half, go_left, 0, GAP)
        to_the_left, to_the_right = sends(n, i, half)
        copies.append((to_the_left, to_the_right))
        if n > 0:
            need(("w", 1, half))
            to_the_right.start()
            over_rows(half, go_left, GAP)
            over_rows(half, functools.partial(inner, i=i), 0, GAP)
            if n == 1:
                @pl.when(last)
                def _():
                    pl.semaphore_wait(ready.at[0], 1)
                    copies[0][0].start()
            to_the_left.start()
        else:
            waits = 2 + has_above.astype(jnp.int32) + detour_over.astype(jnp.int32)
            waits = waits + (feeder & has_below).astype(jnp.int32)
            pl.semaphore_wait(barrier, jnp.where(last, 1, waits))
            to_the_right.start()
            over_rows(half, go_left, GAP)
            need(("w", 1, half))
            over_rows(half, functools.partial(inner, i=i), 0, GAP)

            @pl.when(jnp.logical_not(last))
            def _():
                to_the_left.start()

            @pl.when(feeder)
            def _():
                tell(ready.at[0], {"mom": right})

            @pl.when(feeder & has_below)
            def _():
                tell(ready.at[1], {"energy": group - 1})

            @pl.when(direct_up & jnp.logical_not(last))
            def _():
                below.start()

            @pl.when(detour_up)
            def _():
                out_of_way.start()

            @pl.when(jnp.logical_not(has_below))
            def _():
                slots[0] = jnp.zeros((2, NO, NO), jnp.bfloat16)


    for n, (i, half) in enumerate(CHUNKS):
        over_rows(half, functools.partial(inner, i=i), GAP)

    for n, (i, half) in enumerate(CHUNKS):
        for copy in copies[n]:
            copy.wait_recv()

        def final(r, i=i):
            for c in range(2):
                rows = pl.ds(r, STEP)
                total = own[i, c, rows, :] + from_right[i, c, rows, :].astype(jnp.float32)
                total = total + from_left[i, c, rows, :].astype(jnp.float32)
                out[i, c, rows, :] = total.astype(jnp.bfloat16)

        over_rows(half, final)

    for pair in copies:
        for copy in pair:
            copy.wait_send()

    @pl.when(direct_up)
    def _():
        below.wait_send()

    @pl.when(detour_up)
    def _():
        out_of_way.wait_send()

    @pl.when(detour_over)
    def _():
        back.wait_send()


def body(green, coupling, phonon, shift):
    block = (E_OUT, 2, NO, NO)
    n = len(CHUNKS)
    result = pl.pallas_call(
        kernel,
        out_shape=jax.ShapeDtypeStruct(block, jnp.bfloat16),
        in_specs=[pl.BlockSpec(memory_space=pltpu.HBM)] * 4,
        out_specs=pl.BlockSpec(memory_space=pltpu.VMEM),
        scratch_shapes=[
            pltpu.SMEM((MODES, NOFF), jnp.int32),
            pltpu.VMEM((E_OUT + 1, 2, NO, NO), jnp.bfloat16),
            pltpu.VMEM((MODES, NO, NO), jnp.bfloat16),
            pltpu.VMEM((NOFF, MODES * 2, NO, NO), jnp.bfloat16),
            pltpu.VMEM((E_OUT + 1, MODES, 2, NO, NO), jnp.float32),
            pltpu.VMEM(block, jnp.bfloat16),
            pltpu.VMEM(block, jnp.bfloat16),
            pltpu.VMEM(block, jnp.bfloat16),
            pltpu.VMEM(block, jnp.bfloat16),
            pltpu.VMEM(block, jnp.float32),
            pltpu.VMEM((2, NO, NO), jnp.bfloat16),
            pltpu.SemaphoreType.DMA((E_OUT + 2 + 2 * NOFF,)),
            pltpu.SemaphoreType.DMA((2,)),
            pltpu.SemaphoreType.DMA((3,)),
            pltpu.SemaphoreType.REGULAR((3,)),
            pltpu.SemaphoreType.DMA((n,)),
            pltpu.SemaphoreType.DMA((n,)),
            pltpu.SemaphoreType.DMA((n,)),
            pltpu.SemaphoreType.DMA((n,)),
        ],
        compiler_params=pltpu.CompilerParams(
            collective_id=0, has_side_effects=True, vmem_limit_bytes=VMEM_LIMIT
        ),
    )(
        pltpu.with_memory_space_constraint(green.reshape(block), pltpu.HBM),
        pltpu.with_memory_space_constraint(coupling, pltpu.HBM),
        pltpu.with_memory_space_constraint(phonon.reshape(NOFF, MODES * 2, NO, NO), pltpu.HBM),
        pltpu.with_memory_space_constraint(shift.T, pltpu.HBM),
    )
    return result.reshape((1, 1) + block)


def solution(mesh):
    placed = (P("mom", "energy", None, None, None, None), P(), P(), P())
    return jax.shard_map(
        body,
        mesh=mesh,
        in_specs=placed,
        out_specs=P("mom", "energy", None, None, None, None),
        check_vma=False,
    )
```
